32 devices in a mesh: dp: 16 (over z, y, core), tensor: 2 (over x).
Axes of the slice: x: 2, y: 2, z: 4, core: 2. Of those that a mesh axis runs over, the one named last changes fastest.
Arguments:
- tokens: bfloat16 [2, 16384, 768], P(None, 'dp'), may hold values from -6 to 6
- order: int32 [2, 16384], P(None, 'dp'), may hold values from 0 to 16383, as said below
- lengths: int32 [2, 16, 4], P(None, 'dp'), may hold values from 0 to 1024, as said below
- attn_weight: bfloat16 [768, 3, 768], P('dp', None, 'tensor'), may hold values from -0.21875 to 0.21875
- attn_bias: bfloat16 [2, 768], P(None, 'tensor'), may hold values from -3 to 3
- out_weight: bfloat16 [768, 768], P('tensor', 'dp'), may hold values from -4 to 4
- out_bias: bfloat16 [768], replicated, may hold values from -3 to 3
- gain_one: bfloat16 [768], replicated, may hold values from 0.5 to 1.5
- shift_one: bfloat16 [768], replicated, may hold values from -2 to 2
- up_weight: bfloat16 [768, 3072], P('dp', 'tensor'), may hold values from -0.21875 to 0.21875
- up_bias: bfloat16 [3072], P('tensor'), may hold values from -3 to 3
- down_weight: bfloat16 [3072, 768], P('tensor', 'dp'), may hold values from -0.109375 to 0.109375
- down_bias: bfloat16 [768], replicated, may hold values from -3 to 3
- gain_two: bfloat16 [768], replicated, may hold values from 0.5 to 1.5
- shift_two: bfloat16 [768], replicated, may hold values from -2 to 2
- cotangent: bfloat16 [2, 16384, 768], P(None, 'dp'), may hold values from -6 to 6
Outputs:
- output: bfloat16 [2, 16384, 768], P(None, 'dp')
- input_grad: bfloat16 [2, 16384, 768], P(None, 'dp')
- grad_attention: float32 [768, 3, 768], P('dp', None, 'tensor')
- grad_attnbias: float32 [2, 768], P(None, 'tensor')
- grad_outproj: float32 [768, 768], P('tensor', 'dp')
- grad_outbias: float32 [768], replicated
- grad_gainone: float32 [768], replicated
- grad_shiftone: float32 [768], replicated
- grad_upproj: float32 [768, 3072], P('dp', 'tensor')
- grad_upbias: float32 [3072], P('tensor')
- grad_downproj: float32 [3072, 768], P('tensor', 'dp')
- grad_downbias: float32 [768], replicated
- grad_gaintwo: float32 [768], replicated
- grad_shifttwo: float32 [768], replicated
The draws below stay inside these ranges and needn't reach their ends.
Inputs may be any that keep to these rules, and one draw needn't show every extreme that they name: In each micro-batch order is a permutation of the 16384 rows; the 1024 given rows on each device of dp go to exactly 64 rows of each device's block of the layout. lengths[m, d] are the sequences of block (m, d), packed from row 0; a zero is an empty slot; each block's lengths sum to 512 or more and at most 1024; in every draw some block holds a single sequence of 1024 rows.
All inputs are finite; a program needn't handle non-finite values.
Results may differ from the reference program's by a relative error of at most 0.018.
Values may be sent and summed in bfloat16 or wider, within the bound.
A program may use at most 256 MiB of HBM per device.

```python
import jax
import jax.numpy as jnp
from jax import lax

D = 768
HEADS = 12
FF = 3072
HEAD_DIM = 64
CAP = 1024
MB = 2
SLOTS = 4
ROWS = 16384
N_DP = 16


def draw_order(key, part):
    group_rows = CAP // N_DP

    def one_batch(batch_key):
        key_dest, key_src = jax.random.split(batch_key)
        dest_perm = jax.vmap(lambda sub_key: jax.random.permutation(sub_key, CAP))(jax.random.split(key_dest, N_DP))
        src_perm = jax.vmap(lambda sub_key: jax.random.permutation(sub_key, CAP))(jax.random.split(key_src, N_DP))
        item_ids = jnp.arange(CAP, dtype=jnp.int32)
        dest_dev = item_ids // group_rows
        member = item_ids % group_rows
        sources = jnp.arange(N_DP, dtype=jnp.int32)[:, None]
        target_rows = dest_dev[None, :] * CAP + dest_perm[dest_dev[None, :], sources * group_rows + member[None, :]]
        source_rows = jnp.broadcast_to(sources, (N_DP, CAP))
        placed = jnp.zeros((N_DP, CAP), jnp.int32).at[source_rows, src_perm].set(target_rows.astype(jnp.int32))
        return placed.reshape(N_DP * CAP)
    return jax.vmap(one_batch)(jax.random.split(key, MB)).astype(jnp.int32)


def draw_lengths(key, part):
    key_used, key_cuts, key_batch, key_dev = jax.random.split(key, 4)
    used_rows = jax.random.randint(key_used, (MB, N_DP), CAP // 2, CAP + 1)
    raw_cuts = jax.random.randint(key_cuts, (MB, N_DP, SLOTS - 1), 0, CAP + 1)
    cut_rows = jnp.sort(raw_cuts * used_rows[:, :, None] // CAP, axis=-1)
    edges = jnp.concatenate([jnp.zeros((MB, N_DP, 1), jnp.int32), cut_rows, used_rows[:, :, None]], axis=-1)
    seq_lens = edges[:, :, 1:] - edges[:, :, :-1]
    pick_batch = jax.random.randint(key_batch, (), 0, MB)
    pick_dev = jax.random.randint(key_dev, (), 0, N_DP)
    single = jnp.zeros((SLOTS,), jnp.int32).at[0].set(CAP)
    chosen = (jnp.arange(MB)[:, None] == pick_batch) & (jnp.arange(N_DP)[None, :] == pick_dev)
    return jnp.where(chosen[:, :, None], single[None, None, :], seq_lens).astype(jnp.int32)


def block_levels(key, dims, cuts, low, high):
    level = 1.0
    for axis_at, parts in cuts:
        draws = jax.random.uniform(jax.random.fold_in(jax.random.fold_in(key, 6), axis_at), (parts,), jnp.float32, low / len(cuts), high / len(cuts))
        level = level * jnp.repeat(jnp.exp(draws), dims[axis_at] // parts).reshape((-1,) + (1,) * (len(dims) - 1 - axis_at))
    return level


def noise(key, dims, width, bound, cuts=(), kind=jnp.bfloat16):
    level = block_levels(key, dims, cuts, -0.22, 0.18) if cuts else 1.0
    values = jax.random.normal(key, dims, jnp.float32) * width * level
    return jnp.minimum(jnp.maximum(values, -bound), bound).astype(kind)


def setup_inputs(seed: int = 0) -> dict:
    streams_of = jax.random.split(jax.random.key(seed), 17)
    tokens = noise(streams_of[0], (MB, ROWS, D), 1.0, 6.0, ((1, 16),))
    order = draw_order(jax.random.fold_in(streams_of[16], 71), 0)
    lengths = draw_lengths(jax.random.fold_in(streams_of[16], 71), 0)
    attn_weight = noise(streams_of[3], (D, 3, D), D ** -0.5, 0.21875, ((0, 16), (2, 2)))
    attn_bias = noise(streams_of[4], (2, D), 0.5, 3.0, ((1, 2),))
    out_weight = noise(streams_of[5], (D, D), (max(1, 3 * D // CAP)) ** -0.5, 4.0, ((0, 2), (1, 16)))
    out_bias = noise(streams_of[6], (D,), 0.5, 3.0)
    gain_one = jnp.clip(1.0 + 0.1 * jax.random.normal(streams_of[7], (D,), jnp.float32), 0.5, 1.5).astype(jnp.bfloat16)
    shift_one = noise(streams_of[8], (D,), 0.3, 2.0)
    up_weight = noise(streams_of[9], (D, FF), D ** -0.5, 0.21875, ((0, 16), (1, 2)))
    up_bias = noise(streams_of[10], (FF,), 0.5, 3.0, ((0, 2),))
    down_weight = noise(streams_of[11], (FF, D), FF ** -0.5, 0.109375, ((0, 2), (1, 16)))
    down_bias = noise(streams_of[12], (D,), 0.5, 3.0)
    gain_two = jnp.clip(1.0 + 0.1 * jax.random.normal(streams_of[13], (D,), jnp.float32), 0.5, 1.5).astype(jnp.bfloat16)
    shift_two = noise(streams_of[14], (D,), 0.3, 2.0)
    cotangent = noise(streams_of[15], (MB, ROWS, D), 1.0, 6.0, ((1, 16),))
    return dict(tokens=tokens, order=order, lengths=lengths, attn_weight=attn_weight, attn_bias=attn_bias, out_weight=out_weight, out_bias=out_bias, gain_one=gain_one, shift_one=shift_one, up_weight=up_weight, up_bias=up_bias, down_weight=down_weight, down_bias=down_bias, gain_two=gain_two, shift_two=shift_two, cotangent=cotangent)


@jax.custom_vjp
def low(v):
    return lax.optimization_barrier(v.astype(jnp.bfloat16)).astype(jnp.float32)

@jax.custom_vjp
def low_back(v):
    return v

def low_keep(v):
    return (low(v), None)

def low_pass(kept, grad):
    return (grad,)

def back_keep(v):
    return (v, None)

def back_low(kept, grad):
    return (low(grad),)
low.defvjp(low_keep, low_pass)
low_back.defvjp(back_keep, back_low)
EPSILON = 1e-12
NEGATIVE = -1e+30

def matmul(left, right):
    return jnp.dot(left, right, precision=lax.Precision.HIGHEST)

def normalize(values_in, gain, shift):
    centre = values_in - lax.optimization_barrier(jnp.mean(values_in, axis=-1, keepdims=True))
    spread = lax.optimization_barrier(jnp.mean(centre * centre, axis=-1, keepdims=True))
    return centre * lax.rsqrt(spread + EPSILON) * gain + shift

def block_forward(params, block_rows, counts):
    attn_w, attn_b, out_w, out_b, gain_a, shift_a, up_w, up_b, down_w, down_b, gain_b, shift_b = params
    places = jnp.arange(CAP, dtype=jnp.int32)
    seg_ends = jnp.cumsum(counts).astype(jnp.int32)
    segment = lax.optimization_barrier(jnp.sum((places[:, None] >= seg_ends[None, :]).astype(jnp.int32), axis=1))
    valid_rows = (places < seg_ends[SLOTS - 1]).astype(jnp.float32)
    query_val = low(low_back(matmul(block_rows, attn_w[:, 0]) + attn_b[0]))
    key_val = low(low_back(matmul(block_rows, attn_w[:, 1])))
    value_val = low(low_back(matmul(block_rows, attn_w[:, 2]) + attn_b[1]))
    query_h = query_val.reshape(CAP, HEADS, HEAD_DIM)
    key_h = key_val.reshape(CAP, HEADS, HEAD_DIM)
    value_h = value_val.reshape(CAP, HEADS, HEAD_DIM)
    scores = jnp.einsum('qhd,khd->hqk', query_h, key_h, precision=lax.Precision.HIGHEST) * HEAD_DIM ** (-0.5)
    scores = low_back(scores)
    same_seg = segment[:, None] == segment[None, :]
    scores = jnp.where(same_seg[None, :, :], scores, NEGATIVE)
    attn_probs = low(jax.nn.softmax(scores, axis=-1))
    context = jnp.einsum('hqk,khd->qhd', attn_probs, value_h, precision=lax.Precision.HIGHEST).reshape(CAP, D)
    context = low(low_back(context))
    attended = low_back(matmul(context, out_w))
    hidden = low(normalize(block_rows + attended + out_b, gain_a, shift_a))
    up_value = low_back(matmul(hidden, up_w) + up_b)
    active = low(jax.nn.gelu(up_value, approximate=False))
    branch = low_back(matmul(active, down_w))
    return normalize(hidden + branch + down_b, gain_b, shift_b) * valid_rows[:, None]

def forward(params, layout_rows, lengths):
    flat_rows = layout_rows.reshape(MB * N_DP, CAP, D)
    flat_counts = lengths.reshape(MB * N_DP, SLOTS)
    checked = jax.checkpoint(block_forward)

    def scan_step(carry_val, block_item):
        return (carry_val, checked(params, block_item[0], block_item[1]))
    _, result = lax.scan(scan_step, jnp.float32(0.0), (flat_rows, flat_counts))
    return result.reshape(MB, ROWS, D)

def reference(tokens, order, lengths, attn_weight, attn_bias, out_weight, out_bias, gain_one, shift_one, up_weight, up_bias, down_weight, down_bias, gain_two, shift_two, cotangent):
    params = tuple((tensor_in.astype(jnp.float32) for tensor_in in (attn_weight, attn_bias, out_weight, out_bias, gain_one, shift_one, up_weight, up_bias, down_weight, down_bias, gain_two, shift_two)))
    batch_idx = jnp.arange(MB, dtype=jnp.int32)[:, None]
    layout_rows = jnp.zeros((MB, ROWS, D), jnp.float32).at[batch_idx, order].set(tokens.astype(jnp.float32))
    layout_cot = jnp.zeros((MB, ROWS, D), jnp.float32).at[batch_idx, order].set(cotangent.astype(jnp.float32))
    outputs, pullback = jax.vjp(lambda weights_in, rows_in: forward(weights_in, rows_in, lengths), params, layout_rows)
    param_grads, rows_grad = pullback(layout_cot)
    output = outputs[batch_idx, order].astype(jnp.bfloat16)
    input_grad = rows_grad[batch_idx, order].astype(jnp.bfloat16)
    return (output, input_grad, param_grads[0], param_grads[1], param_grads[2], param_grads[3], param_grads[4], param_grads[5], param_grads[6], param_grads[7], param_grads[8], param_grads[9], param_grads[10], param_grads[11])
```

```python
import functools

import jax
import jax.numpy as jnp
from jax import lax
from jax.experimental import pallas as pl
from jax.experimental.pallas import tpu as pltpu
from jax.sharding import PartitionSpec as P

HEADS = 12
EPSILON = 1e-12
NEGATIVE = -1e30
SQRT_HALF = 0.7071067811865476
INV_ROOT_TAU = 0.3989422804014327
LANES = 128
F32 = jnp.float32
BF16 = jnp.bfloat16


def dot(a, b, dims=((1,), (0,)), out=F32):
    return lax.dot_general(a, b, (dims, ((), ())), preferred_element_type=out)


NT = ((1,), (1,))
TN = ((0,), (0,))


def three_parts(value):
    high = value.astype(BF16).astype(F32)
    rest = value - high
    middle = rest.astype(BF16).astype(F32)
    return high, middle, rest - middle


def attend_kernel(slots, span, q_ref, k_ref, v_ref, tagq_ref, tagk_ref, c_ref, keep_ref):
    rows = q_ref.shape[1]
    half = LANES // 2
    lane = lax.broadcasted_iota(jnp.int32, (1, LANES), 1)
    own = [lane < half, lane >= half]
    tag = lane % half
    tags_k = tagk_ref[...]
    keys = [jnp.where(own[h], k_ref[0], tags_k) for h in range(2)]
    ones = jnp.ones((1, LANES), BF16)
    values = [jnp.where(own[h], v_ref[0], ones) for h in range(2)]

    def step(i, carry):
        at = pl.ds(pl.multiple_of(i * span, span), span)
        q = q_ref[0, at] * jnp.asarray(half ** (-0.5), BF16)
        tags_q = tagq_ref[at]
        outs = []
        for h in range(2):
            qa = jnp.where(own[h], q, tags_q)
            s = dot(qa, keys[h], NT)
            top = jnp.max(s, axis=-1, keepdims=True)
            p = jnp.exp(s - top).astype(BF16)
            o = dot(p, values[h])
            total = pltpu.roll(o, half, 1)
            outs.append(o / jnp.where(own[h], total, 1.0))
            log_sum = top + jnp.log(jnp.where(own[h], 1.0, o))
            parts = three_parts(-log_sum)
            kept = qa.astype(F32)
            for n in range(3):
                kept = jnp.where(~own[h] & (tag == slots + n), parts[n], kept)
            keep_ref[h, at] = kept.astype(BF16)
        c_ref[0, at] = jnp.where(own[0], outs[0], outs[1]).astype(BF16)
        return carry

    lax.fori_loop(0, rows // span, step, 0)


def attend(qkv, tags_q, tags_k, slots):
    halves, rows, width = qkv.shape
    local = width // 3
    pairs = local // LANES
    span = min(256, rows)

    def column(n):
        return pl.BlockSpec((1, rows, LANES), lambda t, p: (t, 0, n * pairs + p))

    whole = pl.BlockSpec((rows, LANES), lambda t, p: (0, 0))
    return pl.pallas_call(
        functools.partial(attend_kernel, slots, span),
        grid=(halves, pairs),
        in_specs=[column(0), column(1), column(2), whole, whole],
        out_specs=[
            pl.BlockSpec((1, rows, LANES), lambda t, p: (t, 0, p)),
            pl.BlockSpec((2, rows, LANES), lambda t, p: (t * pairs + p, 0, 0)),
        ],
        out_shape=[
            jax.ShapeDtypeStruct((halves, rows, local), BF16),
            jax.ShapeDtypeStruct((halves * pairs * 2, rows, LANES), BF16),
        ],
        name="attend",
    )(qkv, qkv, qkv, tags_q, tags_k)


def attend_back_kernel(span, keep_ref, k_ref, v_ref, c_ref, g_ref, tagk_ref, dq_ref, dk_ref, dv_ref, acc_k, acc_v):
    rows = k_ref.shape[1]
    half = LANES // 2
    lane = lax.broadcasted_iota(jnp.int32, (1, LANES), 1)
    own = [lane < half, lane >= half]
    tag = lane % half
    tags_k = tagk_ref[...]
    keys = [jnp.where(own[h], k_ref[0], tags_k) for h in range(2)]
    ones = jnp.ones((1, LANES), BF16)
    values = [jnp.where(own[h], v_ref[0], ones) for h in range(2)]
    plain = k_ref[0]
    scale = half ** (-0.5)
    acc_k[...] = jnp.zeros_like(acc_k)
    acc_v[...] = jnp.zeros_like(acc_v)

    def step(i, carry):
        at = pl.ds(pl.multiple_of(i * span, span), span)
        g = g_ref[0, at]
        prod = g.astype(F32) * c_ref[0, at].astype(F32)
        grads = []
        for h in range(2):
            delta = jnp.sum(jnp.where(own[h], prod, 0.0), axis=-1, keepdims=True)
            parts = three_parts(-delta)
            ga = jnp.where(own[h], g.astype(F32), 0.0)
            for n in range(3):
                ga = jnp.where(~own[h] & (tag == n), parts[n], ga)
            ga = ga.astype(BF16)
            qa = keep_ref[h, at]
            st = dot(keys[h], qa, NT)
            pt = jnp.exp(st)
            dpt = dot(values[h], ga, NT)
            dst = (pt * dpt).astype(BF16)
            acc_v[h] += dot(pt.astype(BF16), g)
            acc_k[h] += dot(dst, qa)
            grads.append(dot(dst, plain, TN))
        dq_ref[0, at] = (jnp.where(own[0], grads[0], grads[1]) * scale).astype(BF16)
        return carry

    lax.fori_loop(0, rows // span, step, 0)
    dk_ref[0] = jnp.where(own[0], acc_k[0], acc_k[1]).astype(BF16)
    dv_ref[0] = jnp.where(own[0], acc_v[0], acc_v[1]).astype(BF16)


def attend_back(qkv, keep, context, grad_context, tags_k):
    halves, rows, width = qkv.shape
    local = width // 3
    pairs = local // LANES
    span = min(256, rows)

    def column(n):
        return pl.BlockSpec((1, rows, LANES), lambda t, p: (t, 0, n * pairs + p))

    whole = pl.BlockSpec((rows, LANES), lambda t, p: (0, 0))
    return pl.pallas_call(
        functools.partial(attend_back_kernel, span),
        grid=(halves, pairs),
        in_specs=[
            pl.BlockSpec((2, rows, LANES), lambda t, p: (t * pairs + p, 0, 0)),
            column(1),
            column(2),
            column(0),
            column(0),
            whole,
        ],
        out_specs=[column(0)] * 3,
        out_shape=[jax.ShapeDtypeStruct((halves, rows, local), BF16)] * 3,
        scratch_shapes=[pltpu.VMEM((2, rows, LANES), F32)] * 2,
        name="attend_back",
    )(keep, qkv, qkv, context, grad_context, tags_k)


def normalize(values_in, gain, shift):
    centre = values_in - jnp.mean(values_in, axis=-1, keepdims=True)
    inverse = lax.rsqrt(jnp.mean(centre * centre, axis=-1, keepdims=True) + EPSILON)
    normed = centre * inverse
    return (normed * gain.astype(F32) + shift.astype(F32), normed, inverse)


def normalize_back(grad_out, normed, inverse, gain):
    scaled = grad_out * gain.astype(F32)
    centred = (
        scaled
        - jnp.mean(scaled, axis=-1, keepdims=True)
        - normed * jnp.mean(scaled * normed, axis=-1, keepdims=True)
    )
    return (inverse * centred, jnp.sum(grad_out * normed, axis=0), jnp.sum(grad_out, axis=0))


def select(index, data):
    length = data.shape[0]
    pick = (jnp.arange(length, dtype=jnp.int32)[:, None] == index[None, :]).astype(BF16)
    return dot(pick, data).astype(data.dtype)


def select_back(index, data):
    length = data.shape[0]
    pick = (index[:, None] == jnp.arange(length, dtype=jnp.int32)[None, :]).astype(BF16)
    return dot(pick, data).astype(data.dtype)


def per_device(
    tokens, order, lengths, attn_weight, attn_bias, out_weight, out_bias, gain_one, shift_one,
    up_weight, up_bias, down_weight, down_bias, gain_two, shift_two, cotangent,
):
    peers = lax.axis_size("dp")
    partners = lax.axis_size("tensor")
    batches, capacity, model_width = tokens.shape
    group_rows = capacity // peers
    slots = lengths.shape[-1] + 1
    mine = lax.axis_index("tensor")

    shard_rows = attn_weight.shape[0]
    attn_cols = attn_weight.shape[1] * attn_weight.shape[2]
    shard_a = jnp.concatenate([attn_weight.reshape(shard_rows, attn_cols), out_weight.T], axis=1)
    shard_b = jnp.concatenate([up_weight, down_weight.T], axis=1)
    both = ("tensor", "dp")
    full_a = lax.all_gather(shard_a, both, axis=0, tiled=True).reshape(partners, model_width, -1)
    full_b = lax.all_gather(shard_b, both, axis=0, tiled=True).reshape(partners, model_width, -1)
    local_width = out_weight.shape[0]
    hidden_width = up_weight.shape[1]
    full_bias = lax.all_gather(
        jnp.concatenate([attn_bias.reshape(-1), up_bias]).reshape(1, -1), "tensor", axis=0, tiled=True
    ).astype(F32)
    q_bias = full_bias[:, :local_width]
    v_bias = full_bias[:, local_width : 2 * local_width]
    up_full_bias = full_bias[:, 2 * local_width :]

    target_dev = order // capacity
    local_row = order % capacity
    onehot = (target_dev[:, :, None] == jnp.arange(peers, dtype=jnp.int32)).astype(BF16)
    earlier = (jnp.arange(capacity)[:, None] > jnp.arange(capacity)[None, :]).astype(BF16)
    before = jnp.stack([dot(earlier, onehot[m]) for m in range(batches)])
    rank_in = jnp.sum(before * onehot.astype(F32), axis=2).astype(jnp.int32)
    send_slot = target_dev * group_rows + rank_in
    my_slot = lax.dynamic_index_in_dim(send_slot, mine, 0, keepdims=False)
    my_row = lax.dynamic_index_in_dim(local_row, mine, 0, keepdims=False)
    my_tokens = lax.dynamic_index_in_dim(tokens, mine, 0, keepdims=False)
    my_cot = lax.dynamic_index_in_dim(cotangent, mine, 0, keepdims=False)
    my_counts = lax.dynamic_index_in_dim(lengths, mine, 0, keepdims=False)[0]
    shape_three = (peers, group_rows, model_width)
    pick = (jnp.arange(capacity, dtype=jnp.int32)[:, None] == my_slot[None, :])
    send_rows = dot(pick.astype(BF16), my_tokens).astype(BF16).reshape(shape_three)
    send_cot = dot(pick.astype(BF16), my_cot).astype(BF16).reshape(shape_three)
    send_index = jnp.sum(jnp.where(pick, my_row[None, :], 0), axis=1).reshape(peers, group_rows)
    exchange = functools.partial(
        lax.all_to_all, axis_name="dp", split_axis=0, concat_axis=0, tiled=True
    )
    recv_index = exchange(send_index).reshape(capacity)
    recv_rows = exchange(send_rows).reshape(capacity, model_width)
    recv_cot = exchange(send_cot).reshape(capacity, model_width)
    block_rows = select(recv_index, recv_rows)
    block_cot = select(recv_index, recv_cot)

    places = jnp.arange(capacity, dtype=jnp.int32)
    seg_ends = jnp.cumsum(my_counts)
    segment = jnp.sum((places[:, None] >= seg_ends[None, :]).astype(jnp.int32), axis=1)
    valid_rows = (places < seg_ends[-1]).astype(F32)
    tag = jnp.arange(LANES, dtype=jnp.int32) % (LANES // 2)
    same = segment[:, None] == tag[None, :]
    tags_q = same.astype(BF16)
    tags_k = jnp.where(
        tag[None, :] < slots, jnp.where(same, 0.0, NEGATIVE), (tag[None, :] < slots + 3).astype(F32)
    ).astype(BF16)

    mixed_bias = jnp.concatenate([q_bias, jnp.zeros_like(q_bias), v_bias], axis=1)
    qkv = jnp.stack(
        [
            (dot(block_rows, full_a[t, :, :attn_cols]) + mixed_bias[t]).astype(BF16)
            for t in range(partners)
        ]
    )
    context, keep = attend(qkv, tags_q, tags_k, slots)
    attended = sum(dot(context[t], full_a[t, :, attn_cols:], NT) for t in range(partners))
    first, normed_one, inverse_one = normalize(
        block_rows.astype(F32) + attended + out_bias, gain_one, shift_one
    )
    hidden = first.astype(BF16)
    up_value = [dot(hidden, full_b[t, :, :hidden_width]) + up_full_bias[t] for t in range(partners)]
    active = [jax.nn.gelu(u, approximate=False).astype(BF16) for u in up_value]
    branch = sum(dot(active[t], full_b[t, :, hidden_width:], NT) for t in range(partners))
    second, normed_two, inverse_two = normalize(
        hidden.astype(F32) + branch + down_bias, gain_two, shift_two
    )
    layout_out = (second * valid_rows[:, None]).astype(BF16)

    grad_y = block_cot.astype(F32) * valid_rows[:, None]
    grad_second, gain_two_part, shift_two_part = normalize_back(
        grad_y, normed_two, inverse_two, gain_two
    )
    grad_branch = grad_second.astype(BF16)
    hidden_terms = 0.0
    up_bias_part = []
    grads_b = []
    for t in range(partners):
        down_part = dot(grad_branch, active[t], TN, BF16)
        grad_active = dot(grad_branch, full_b[t, :, hidden_width:])
        u = up_value[t]
        slope = 0.5 * (1.0 + lax.erf(u * SQRT_HALF)) + u * jnp.exp(-0.5 * u * u) * INV_ROOT_TAU
        grad_up = (grad_active * slope).astype(BF16)
        up_part = dot(hidden, grad_up, TN, BF16)
        up_bias_part.append(jnp.sum(grad_up.astype(F32), axis=0))
        hidden_terms = hidden_terms + dot(grad_up, full_b[t, :, :hidden_width], NT)
        grads_b.append(jnp.concatenate([up_part, down_part], axis=1))
    scatter = functools.partial(
        lax.psum_scatter, axis_name=both, scatter_dimension=0, tiled=True
    )
    share_b = scatter(jnp.concatenate(grads_b, axis=0)).astype(F32)
    grad_hidden = grad_second + hidden_terms
    grad_first, gain_one_part, shift_one_part = normalize_back(
        grad_hidden, normed_one, inverse_one, gain_one
    )
    grad_attended = grad_first.astype(BF16)
    grad_context = jnp.stack(
        [dot(grad_attended, full_a[t, :, attn_cols:], out=F32).astype(BF16) for t in range(partners)]
    )
    grad_q, grad_k, grad_v = attend_back(qkv, keep, context, grad_context, tags_k)
    input_terms = grad_first
    grads_a = []
    for t in range(partners):
        grad_mixed = jnp.concatenate([grad_q[t], grad_k[t], grad_v[t]], axis=1)
        out_part = dot(grad_attended, context[t], TN, BF16)
        attn_part = dot(block_rows, grad_mixed, TN, BF16)
        input_terms = input_terms + dot(grad_mixed, full_a[t, :, :attn_cols], NT)
        grads_a.append(jnp.concatenate([attn_part, out_part], axis=1))
    share_a = scatter(jnp.concatenate(grads_a, axis=0)).astype(F32)
    layout_grad = input_terms.astype(BF16)
    small = jnp.concatenate(
        [
            jnp.sum(grad_q.astype(F32), axis=1).reshape(-1),
            jnp.sum(grad_v.astype(F32), axis=1).reshape(-1),
            jnp.concatenate(up_bias_part),
            jnp.sum(grad_first, axis=0),
            gain_one_part,
            shift_one_part,
            jnp.sum(grad_second, axis=0),
            gain_two_part,
            shift_two_part,
        ]
    )
    small = lax.psum(small.reshape(-1, model_width), ("dp", "tensor")).reshape(-1)
    width = model_width
    ends = [0, width, 2 * width]
    q_sum = small[:width].reshape(partners, -1)
    v_sum = small[width : 2 * width].reshape(partners, -1)
    base = 2 * width + partners * hidden_width
    u_sum = small[2 * width : base].reshape(partners, -1)
    rest = small[base:].reshape(6, width)
    own = functools.partial(lax.dynamic_index_in_dim, index=mine, axis=0, keepdims=False)

    back_out = exchange(select_back(recv_index, layout_out).reshape(shape_three))
    back_grad = exchange(select_back(recv_index, layout_grad).reshape(shape_three))
    swap = [(i, (i + 1) % partners) for i in range(partners)]

    def home(back):
        here = back.reshape(capacity, model_width)
        there = lax.ppermute(here, "tensor", swap)
        rows = []
        for m in range(batches):
            rows.append(select_back(send_slot[m], jnp.where(mine == m, here, there)))
        return jnp.stack(rows)

    output = home(back_out)
    input_grad = home(back_grad)
    return (
        output,
        input_grad,
        share_a[:, :attn_cols].reshape(shard_rows, 3, local_width),
        jnp.stack([own(q_sum), own(v_sum)]),
        share_a[:, attn_cols:].T,
        rest[0],
        rest[1],
        rest[2],
        share_b[:, :hidden_width],
        own(u_sum),
        share_b[:, hidden_width:].T,
        rest[3],
        rest[4],
        rest[5],
    )


def solution(mesh):
    in_specs = (
        P(None, "dp", None),
        P(None, "dp"),
        P(None, "dp", None),
        P("dp", None, "tensor"),
        P(None, "tensor"),
        P("tensor", "dp"),
        P(),
        P(),
        P(),
        P("dp", "tensor"),
        P("tensor"),
        P("tensor", "dp"),
        P(),
        P(),
        P(),
        P(None, "dp", None),
    )
    out_specs = (
        P(None, "dp", None),
        P(None, "dp", None),
        P("dp", None, "tensor"),
        P(None, "tensor"),
        P("tensor", "dp"),
        P(),
        P(),
        P(),
        P("dp", "tensor"),
        P("tensor"),
        P("tensor", "dp"),
        P(),
        P(),
        P(),
    )
    return jax.shard_map(
        per_device, mesh=mesh, in_specs=in_specs, out_specs=out_specs, check_vma=False
    )
```

```python
import functools

import jax
import jax.numpy as jnp
from jax import lax
from jax.experimental import pallas as pl
from jax.experimental.pallas import tpu as pltpu
from jax.sharding import PartitionSpec as P

HEADS = 12
EPSILON = 1e-12
NEGATIVE = -1e30
SQRT_HALF = 0.7071067811865476
INV_ROOT_TAU = 0.3989422804014327
LANES = 128
F32 = jnp.float32
BF16 = jnp.bfloat16


def dot(a, b, dims=((1,), (0,)), out=F32):
    return lax.dot_general(a, b, (dims, ((), ())), preferred_element_type=out)


NT = ((1,), (1,))
TN = ((0,), (0,))


def three_parts(value):
    high = value.astype(BF16).astype(F32)
    rest = value - high
    middle = rest.astype(BF16).astype(F32)
    return high, middle, rest - middle


def attend_kernel(slots, span, q_ref, k_ref, v_ref, tagq_ref, tagk_ref, c_ref, keep_ref):
    rows = q_ref.shape[1]
    half = LANES // 2
    lane = lax.broadcasted_iota(jnp.int32, (1, LANES), 1)
    own = [lane < half, lane >= half]
    tag = lane % half
    tags_k = tagk_ref[...]
    keys = [jnp.where(own[h], k_ref[0], tags_k) for h in range(2)]
    ones = jnp.ones((1, LANES), BF16)
    values = [jnp.where(own[h], v_ref[0], ones) for h in range(2)]

    def step(i, carry):
        at = pl.ds(pl.multiple_of(i * span, span), span)
        q = q_ref[0, at] * jnp.asarray(half ** (-0.5), BF16)
        tags_q = tagq_ref[at]
        outs = []
        for h in range(2):
            qa = jnp.where(own[h], q, tags_q)
            s = dot(qa, keys[h], NT)
            top = jnp.max(s, axis=-1, keepdims=True)
            p = jnp.exp(s - top).astype(BF16)
            o = dot(p, values[h])
            total = pltpu.roll(o, half, 1)
            outs.append(o / jnp.where(own[h], total, 1.0))
            log_sum = top + jnp.log(jnp.where(own[h], 1.0, o))
            parts = three_parts(-log_sum)
            kept = qa.astype(F32)
            for n in range(3):
                kept = jnp.where(~own[h] & (tag == slots + n), parts[n], kept)
            keep_ref[h, at] = kept.astype(BF16)
        c_ref[0, at] = jnp.where(own[0], outs[0], outs[1]).astype(BF16)
        return carry

    lax.fori_loop(0, rows // span, step, 0)


def attend(qkv, tags_q, tags_k, slots):
    halves, rows, width = qkv.shape
    local = width // 3
    pairs = local // LANES
    span = min(256, rows)

    def column(n):
        return pl.BlockSpec((1, rows, LANES), lambda t, p: (t, 0, n * pairs + p))

    whole = pl.BlockSpec((rows, LANES), lambda t, p: (0, 0))
    return pl.pallas_call(
        functools.partial(attend_kernel, slots, span),
        grid=(halves, pairs),
        in_specs=[column(0), column(1), column(2), whole, whole],
        out_specs=[
            pl.BlockSpec((1, rows, LANES), lambda t, p: (t, 0, p)),
            pl.BlockSpec((2, rows, LANES), lambda t, p: (t * pairs + p, 0, 0)),
        ],
        out_shape=[
            jax.ShapeDtypeStruct((halves, rows, local), BF16),
            jax.ShapeDtypeStruct((halves * pairs * 2, rows, LANES), BF16),
        ],
        name="attend",
    )(qkv, qkv, qkv, tags_q, tags_k)


def attend_back_kernel(span, keep_ref, k_ref, v_ref, c_ref, g_ref, tagk_ref, dq_ref, dk_ref, dv_ref, acc_k, acc_v):
    rows = k_ref.shape[1]
    half = LANES // 2
    lane = lax.broadcasted_iota(jnp.int32, (1, LANES), 1)
    own = [lane < half, lane >= half]
    tag = lane % half
    tags_k = tagk_ref[...]
    keys = [jnp.where(own[h], k_ref[0], tags_k) for h in range(2)]
    ones = jnp.ones((1, LANES), BF16)
    values = [jnp.where(own[h], v_ref[0], ones) for h in range(2)]
    plain = k_ref[0]
    scale = half ** (-0.5)
    acc_k[...] = jnp.zeros_like(acc_k)
    acc_v[...] = jnp.zeros_like(acc_v)

    def step(i, carry):
        at = pl.ds(pl.multiple_of(i * span, span), span)
        g = g_ref[0, at]
        prod = g.astype(F32) * c_ref[0, at].astype(F32)
        grads = []
        for h in range(2):
            delta = jnp.sum(jnp.where(own[h], prod, 0.0), axis=-1, keepdims=True)
            parts = three_parts(-delta)
            ga = jnp.where(own[h], g.astype(F32), 0.0)
            for n in range(3):
                ga = jnp.where(~own[h] & (tag == n), parts[n], ga)
            ga = ga.astype(BF16)
            qa = keep_ref[h, at]
            st = dot(keys[h], qa, NT)
            pt = jnp.exp(st)
            dpt = dot(values[h], ga, NT)
            dst = (pt * dpt).astype(BF16)
            acc_v[h] += dot(pt.astype(BF16), g)
            acc_k[h] += dot(dst, qa)
            grads.append(dot(dst, plain, TN))
        dq_ref[0, at] = (jnp.where(own[0], grads[0], grads[1]) * scale).astype(BF16)
        return carry

    lax.fori_loop(0, rows // span, step, 0)
    dk_ref[0] = jnp.where(own[0], acc_k[0], acc_k[1]).astype(BF16)
    dv_ref[0] = jnp.where(own[0], acc_v[0], acc_v[1]).astype(BF16)


def attend_back(qkv, keep, context, grad_context, tags_k):
    halves, rows, width = qkv.shape
    local = width // 3
    pairs = local // LANES
    span = min(256, rows)

    def column(n):
        return pl.BlockSpec((1, rows, LANES), lambda t, p: (t, 0, n * pairs + p))

    whole = pl.BlockSpec((rows, LANES), lambda t, p: (0, 0))
    return pl.pallas_call(
        functools.partial(attend_back_kernel, span),
        grid=(halves, pairs),
        in_specs=[
            pl.BlockSpec((2, rows, LANES), lambda t, p: (t * pairs + p, 0, 0)),
            column(1),
            column(2),
            column(0),
            column(0),
            whole,
        ],
        out_specs=[column(0)] * 3,
        out_shape=[jax.ShapeDtypeStruct((halves, rows, local), BF16)] * 3,
        scratch_shapes=[pltpu.VMEM((2, rows, LANES), F32)] * 2,
        name="attend_back",
    )(keep, qkv, qkv, context, grad_context, tags_k)


MESH = pl.DeviceIdType.MESH
ANY = pl.BlockSpec(memory_space=pl.ANY)


class Place:
    def __init__(self):
        self.peers = lax.axis_size("dp")
        self.depth = self.peers // 4
        self.dp = lax.axis_index("dp")
        self.x = lax.axis_index("tensor")
        self.core = self.dp % 2
        self.y = (self.dp // 2) % 2
        self.z = self.dp // 4

    def shard(self, a, b, z, core=None):
        core = self.core if core is None else core
        y = (self.y + b * (1 - core) + a * core) % 2
        x = (self.x + b * core + a * (1 - core)) % 2
        return x, (z * 2 + y) * 2 + core

    def device(self, a, b, z):
        x, dp = self.shard(a, b, z)
        return {"dp": dp, "tensor": x}

    def partner(self):
        return {"dp": self.dp + 1 - 2 * self.core, "tensor": self.x}

    def up(self, j):
        return (self.z + j) % self.depth

    def down(self, j):
        return (self.z + self.depth - j) % self.depth


def remote(src, dst, send, recv, device):
    return pltpu.make_async_remote_copy(
        src_ref=src, dst_ref=dst, send_sem=send, recv_sem=recv, device_id=device, device_id_type=MESH
    )


def enter(place, plane):
    barrier = pltpu.get_barrier_semaphore()
    targets = [{"dp": place.dp, "tensor": 1 - place.x}]
    if plane:
        targets += [
            {"dp": (place.dp + j) % place.peers, "tensor": place.x} for j in range(1, place.peers)
        ]
    else:
        targets += [place.partner(), {"dp": (place.z * 2 + 1 - place.y) * 2 + place.core, "tensor": place.x}]
        targets += [place.device(0, 0, place.up(j)) for j in range(1, place.depth)]
    for device in targets:
        pl.semaphore_signal(barrier, inc=1, device_id=device, device_id_type=MESH)
    pl.semaphore_wait(barrier, len(targets))


def gather_steps(place, own, full, send, recv, local):
    n = place.depth

    def at(shard):
        return full.at[shard[0], shard[1]]

    def copy(k, src, shard, device):
        return remote(src, at(shard), send.at[k], recv.at[k], device)

    mine = place.shard(0, 0, place.z)
    first, second, last = n - 1, 2 * n - 1, 4 * n - 1
    to_one, to_two, other = place.device(0, 1, place.z), place.device(1, 0, place.z), place.partner()
    here = pltpu.make_async_copy(own, at(mine), local)
    copies = []

    def go(k, src, shard, device):
        one = copy(k, src, shard, device)
        one.start()
        copies.append(one)

    def begin():
        for j in range(1, n):
            go(j - 1, own, mine, place.device(0, 0, place.up(j)))
        go(first, own, mine, to_one)
        go(second, own, mine, to_two)
        go(last, own, mine, other)
        here.start()

    def line(j):
        shard = place.shard(0, 0, place.down(j))
        copy(j - 1, own, shard, other).wait_recv()
        go(first + j, at(shard), shard, to_one)
        go(second + j, at(shard), shard, to_two)
        go(last + j, at(shard), shard, other)

    def plane_one(j):
        shard = place.shard(0, 1, place.down(j))
        copy(first + j, own, shard, other).wait_recv()
        go(second + n + j, at(shard), shard, to_two)
        go(last + n + j, at(shard), shard, other)

    def plane_two(i, j):
        shard = place.shard(1, i, place.down(j))
        copy(second + i * n + j, own, shard, other).wait_recv()
        go(last + (2 + i) * n + j, at(shard), shard, other)

    def finish():
        for a in range(2):
            for b in range(2):
                for j in range(n):
                    shard = place.shard(a, b, place.down(j), 1 - place.core)
                    copy(last + (a * 2 + b) * n + j, own, shard, other).wait_recv()
        here.wait()
        for one in copies:
            one.wait_send()

    steps = [begin]
    steps += [functools.partial(line, j) for j in range(1, n)]
    steps += [functools.partial(plane_one, j) for j in range(n)]
    steps += [functools.partial(plane_two, i, j) for i in range(2) for j in range(n)]
    return steps + [finish]


def gather_sems(peers):
    return [pltpu.SemaphoreType.DMA((2 * peers - 1,))] * 2 + [pltpu.SemaphoreType.DMA]


def trade_steps(place, blocks, landing, send, recv, local):
    n = place.peers

    def copy(j):
        to = (place.dp + j) % n
        return remote(
            blocks.at[to], landing.at[place.dp], send.at[j], recv.at[j], {"dp": to, "tensor": place.x}
        )

    here = pltpu.make_async_copy(blocks.at[place.dp], landing.at[place.dp], local)

    def begin():
        for j in range(1, n):
            copy(j).start()
        here.start()

    def finish():
        here.wait()
        for j in range(1, n):
            copy(j).wait_recv()
        for j in range(1, n):
            copy(j).wait_send()

    return [begin, finish]


def trade_sems(peers):
    return [pltpu.SemaphoreType.DMA((peers,))] * 2 + [pltpu.SemaphoreType.DMA]


def home_steps(place, blocks, landing, send, recv, local):
    n = place.peers
    across = {"dp": place.dp, "tensor": 1 - place.x}

    def copy(j):
        to = (place.dp + j) % n
        return remote(
            blocks.at[to], landing.at[place.x, place.dp], send.at[j], recv.at[j], {"dp": to, "tensor": place.x}
        )

    def relay(j, src=None):
        at = (place.dp + n - j) % n
        return remote(
            landing.at[place.x, at] if src is None else src, landing.at[place.x, at], send.at[n + j], recv.at[n + j], across
        )

    def relayed(j):
        at = (place.dp + n - j) % n
        return remote(
            landing.at[1 - place.x, at], landing.at[1 - place.x, at], send.at[n + j], recv.at[n + j], across
        )

    here = pltpu.make_async_copy(blocks.at[place.dp], landing.at[place.x, place.dp], local)

    def begin():
        for j in range(1, n):
            copy(j).start()
        here.start()
        relay(0, blocks.at[place.dp]).start()

    def forward(j):
        copy(j).wait_recv()
        relay(j).start()

    def finish():
        here.wait()
        for j in range(n):
            relayed(j).wait_recv()
        for j in range(1, n):
            copy(j).wait_send()
        for j in range(n):
            relay(j).wait_send()

    return [begin] + [functools.partial(forward, j) for j in range(1, n)] + [finish]


def home_sems(peers):
    return [pltpu.SemaphoreType.DMA((2 * peers,))] * 2 + [pltpu.SemaphoreType.DMA]


def add_into(out, out_at, parts, scratch_type=F32):
    width = parts[0][0].shape[-1]
    tile = next(t for t in (512, 384, 256, 128, width) if width % t == 0)

    def body(i, carry):
        columns = pl.ds(pl.multiple_of(i * tile, tile), tile)
        total = None
        for ref, index in parts:
            value = ref[(*index, slice(None), columns)].astype(F32)
            total = value if total is None else total + value
        out[(*out_at, slice(None), columns)] = total.astype(out.dtype)
        return carry

    lax.fori_loop(0, width // tile, body, 0)


def reduce_scratch(peers, rows, width):
    n = peers // 4
    return [
        pltpu.VMEM((4 * n, rows, width), BF16),
        pltpu.VMEM((4 * n, rows, width), BF16),
        pltpu.VMEM((2 * n, rows, width), BF16),
        pltpu.VMEM((n, rows, width), BF16),
        pltpu.VMEM((n, rows, width), BF16),
        pltpu.VMEM((2 * n, rows, width), BF16),
        pltpu.VMEM((n, rows, width), BF16),
        pltpu.VMEM((n, rows, width), BF16),
        pltpu.SemaphoreType.DMA((4 * n,)),
        pltpu.SemaphoreType.DMA((8 * n,)),
        pltpu.SemaphoreType.DMA((8 * n,)),
    ]


def reduce_steps(place, grads, out, own, from_core, from_two, from_one, from_z, for_two, for_one, for_z, load, send, recv):
    n = place.depth
    other = place.partner()
    to_two, to_one = place.device(1, 0, place.z), place.device(0, 1, place.z)
    order = [(1, 1), (1, 0), (0, 1), (0, 0)]

    def slot(a, b, j):
        return (a * 2 + b) * n + j

    def load_own(a, b, j):
        shard = place.shard(a, b, place.up(j))
        k = slot(a, b, j)
        return pltpu.make_async_copy(grads.at[shard[0], shard[1]], own.at[k], load.at[k])

    def to_core(a, b, j):
        shard = place.shard(a, b, place.up(j), 1 - place.core)
        k = slot(a, b, j)
        return remote(grads.at[shard[0], shard[1]], from_core.at[k], send.at[k], recv.at[k], other)

    def send_two(b, j):
        k = b * n + j
        return remote(for_two.at[k], from_two.at[k], send.at[4 * n + k], recv.at[4 * n + k], to_two)

    def send_one(j):
        return remote(for_one.at[j], from_one.at[j], send.at[6 * n + j], recv.at[6 * n + j], to_one)

    def send_z(j):
        device = place.device(0, 0, place.up(j))
        return remote(for_z.at[j], from_z.at[j], send.at[7 * n + j], recv.at[7 * n + j], device)

    def begin():
        for a, b in order:
            for j in range(n):
                to_core(a, b, j).start()
                load_own(a, b, j).start()

    def arrive(a, b, j):
        load_own(a, b, j).wait()
        to_core(a, b, j).wait_recv()

    def two(b, j):
        arrive(1, b, j)
        add_into(for_two, (b * n + j,), [(own, (slot(1, b, j),)), (from_core, (slot(1, b, j),))])
        send_two(b, j).start()

    def one(j):
        arrive(0, 1, j)
        send_two(1, j).wait_recv()
        k = slot(0, 1, j)
        add_into(for_one, (j,), [(own, (k,)), (from_core, (k,)), (from_two, (n + j,))])
        send_one(j).start()

    def along(j):
        arrive(0, 0, j)
        send_two(0, j).wait_recv()
        send_one(j).wait_recv()
        k = slot(0, 0, j)
        parts = [(own, (k,)), (from_core, (k,)), (from_two, (j,)), (from_one, (j,))]
        if j:
            add_into(for_z, (j,), parts)
            send_z(j).start()
            return
        for i in range(1, n):
            send_z(i).wait_recv()
        add_into(out, (), parts + [(from_z, (i,)) for i in range(1, n)])

    def finish():
        for a, b in order:
            for j in range(n):
                to_core(a, b, j).wait_send()
        for b in range(2):
            for j in range(n):
                send_two(b, j).wait_send()
        for j in range(n):
            send_one(j).wait_send()
        for j in range(1, n):
            send_z(j).wait_send()

    steps = [begin]
    steps += [functools.partial(two, 1, j) for j in range(n)]
    steps += [functools.partial(two, 0, j) for j in range(n)]
    steps += [functools.partial(one, (j + 1) % n) for j in range(n)]
    steps += [functools.partial(along, (j + 1) % n) for j in range(n)]
    return steps + [finish]


def total_scratch(peers, shape):
    n = peers // 4
    return [
        pltpu.VMEM((3, *shape), F32),
        pltpu.VMEM((3, *shape), F32),
        pltpu.VMEM((n, *shape), F32),
        pltpu.SemaphoreType.DMA((3 + n,)),
        pltpu.SemaphoreType.DMA((3 + n,)),
    ]


def total_steps(place, small, out, sums, landed, heights, send, recv):
    n = place.depth
    partners = [
        place.partner(),
        {"dp": place.dp, "tensor": 1 - place.x},
        {"dp": (place.z * 2 + 1 - place.y) * 2 + place.core, "tensor": place.x},
    ]

    def copy(k):
        src = small if k == 0 else sums.at[k - 1]
        return remote(src, landed.at[k], send.at[k], recv.at[k], partners[k])

    def lift(j):
        device = place.device(0, 0, place.up(j))
        return remote(sums.at[2], heights.at[place.z], send.at[3 + j], recv.at[3 + j], device)

    def begin():
        copy(0).start()

    def pair(k):
        copy(k).wait_recv()
        sums[k] = (small[...] if k == 0 else sums[k - 1]) + landed[k]
        if k < 2:
            copy(k + 1).start()
            return
        for j in range(1, n):
            lift(j).start()
        heights[place.z] = sums[2]

    def finish():
        for j in range(1, n):
            lift(j).wait_recv()
        total = heights[0]
        for i in range(1, n):
            total = total + heights[i]
        out[...] = total
        for k in range(3):
            copy(k).wait_send()
        for j in range(1, n):
            lift(j).wait_send()

    return [begin] + [functools.partial(pair, k) for k in range(3)] + [finish]


def run(steps):
    for step in steps:
        step()


def head_kernel(rows, cot, index, shard_a, shard_b, bias, got_rows, got_cot, got_index, full_a, full_b, got_bias, *sems):
    place = Place()
    enter(place, True)
    first = trade_steps(place, rows, got_rows, *sems[0:3])
    second = trade_steps(place, index, got_index, *sems[3:6])
    third = trade_steps(place, cot, got_cot, *sems[6:9])
    gather_a = gather_steps(place, shard_a, full_a, *sems[9:12])
    gather_b = gather_steps(place, shard_b, full_b, *sems[12:15])
    swap_send, swap_recv, swap_here = sems[15:18]
    swap = remote(bias, got_bias.at[place.x], swap_send, swap_recv, {"dp": place.dp, "tensor": 1 - place.x})
    keep = pltpu.make_async_copy(bias, got_bias.at[place.x], swap_here)
    second[0]()
    swap.start()
    keep.start()
    gather_a[0]()
    first[0]()
    gather_b[0]()
    third[0]()
    run(gather_a[1:])
    run(gather_b[1:])
    run(first[1:] + second[1:] + third[1:])
    keep.wait()
    swap.wait()


def head(rows, cot, index, shard_a, shard_b, bias, peers):
    def full(shard):
        return jax.ShapeDtypeStruct((2, peers, *shard.shape), shard.dtype)

    def same(block):
        return jax.ShapeDtypeStruct(block.shape, block.dtype)

    return pl.pallas_call(
        head_kernel,
        in_specs=[ANY] * 6,
        out_specs=[ANY] * 6,
        out_shape=[same(rows), same(cot), same(index), full(shard_a), full(shard_b), jax.ShapeDtypeStruct((2, *bias.shape), bias.dtype)],
        scratch_shapes=trade_sems(peers) * 3 + gather_sems(peers) * 2 + [pltpu.SemaphoreType.DMA] * 3,
        compiler_params=pltpu.CompilerParams(collective_id=1, has_side_effects=True),
        name="head",
    )(rows, cot, index, shard_a, shard_b, bias)


def tail_kernel(count, *refs):
    blocks, small = refs[0:2]
    grads = refs[2 : 2 + count]
    landing, total = refs[2 + count : 4 + count]
    shares = refs[4 + count : 4 + 2 * count]
    scratch = refs[4 + 2 * count :]
    place = Place()
    enter(place, True)
    trade = home_steps(place, blocks, landing, *scratch[0:3])
    sums = total_steps(place, small, total, *scratch[3:8])
    reduce = [
        reduce_steps(place, grads[i], shares[i], *scratch[8 + 11 * i : 19 + 11 * i]) for i in range(count)
    ]
    sums[0]()
    for steps in reduce:
        steps[0]()
    trade[0]()
    for k in range(1, max(len(reduce[0]), len(trade))):
        for steps in reduce:
            run(steps[k : k + 1])
        run(sums[k : k + 1])
        run(trade[k : k + 1])


def tail(blocks, small, grads, peers):
    vmem = pl.BlockSpec(memory_space=pltpu.VMEM)
    shards = [g.shape[2:] for g in grads]
    return pl.pallas_call(
        functools.partial(tail_kernel, len(grads)),
        in_specs=[ANY, vmem] + [ANY] * len(grads),
        out_specs=[ANY, vmem] + [vmem] * len(grads),
        out_shape=[
            jax.ShapeDtypeStruct((2, *blocks.shape), blocks.dtype),
            jax.ShapeDtypeStruct(small.shape, F32),
        ]
        + [jax.ShapeDtypeStruct(s, F32) for s in shards],
        scratch_shapes=home_sems(peers)
        + total_scratch(peers, small.shape)
        + [s for rows, width in shards for s in reduce_scratch(peers, rows, width)],
        compiler_params=pltpu.CompilerParams(collective_id=2, has_side_effects=True),
        name="tail",
    )(blocks, small, *grads)


def normalize(values_in, gain, shift):
    centre = values_in - jnp.mean(values_in, axis=-1, keepdims=True)
    inverse = lax.rsqrt(jnp.mean(centre * centre, axis=-1, keepdims=True) + EPSILON)
    normed = centre * inverse
    return (normed * gain.astype(F32) + shift.astype(F32), normed, inverse)


def normalize_back(grad_out, normed, inverse, gain):
    scaled = grad_out * gain.astype(F32)
    centred = (
        scaled
        - jnp.mean(scaled, axis=-1, keepdims=True)
        - normed * jnp.mean(scaled * normed, axis=-1, keepdims=True)
    )
    return (inverse * centred, jnp.sum(grad_out * normed, axis=0), jnp.sum(grad_out, axis=0))


def select(index, data):
    length = data.shape[0]
    pick = (jnp.arange(length, dtype=jnp.int32)[:, None] == index[None, :]).astype(BF16)
    return dot(pick, data).astype(data.dtype)


def select_back(index, data):
    length = data.shape[0]
    pick = (index[:, None] == jnp.arange(length, dtype=jnp.int32)[None, :]).astype(BF16)
    return dot(pick, data).astype(data.dtype)


def per_device(
    tokens, order, lengths, attn_weight, attn_bias, out_weight, out_bias, gain_one, shift_one,
    up_weight, up_bias, down_weight, down_bias, gain_two, shift_two, cotangent,
):
    peers = lax.axis_size("dp")
    partners = lax.axis_size("tensor")
    batches, capacity, model_width = tokens.shape
    group_rows = capacity // peers
    slots = lengths.shape[-1] + 1
    mine = lax.axis_index("tensor")

    shard_rows = attn_weight.shape[0]
    attn_cols = attn_weight.shape[1] * attn_weight.shape[2]
    shard_a = jnp.concatenate([attn_weight.reshape(shard_rows, attn_cols), out_weight.T], axis=1)
    shard_b = jnp.concatenate([up_weight, down_weight.T], axis=1)
    local_width = out_weight.shape[0]
    hidden_width = up_weight.shape[1]
    bias = jnp.concatenate([attn_bias.reshape(-1), up_bias]).astype(F32)
    bias = jnp.pad(bias, (0, -bias.size % (8 * LANES))).reshape(-1, LANES)

    target_dev = order // capacity
    local_row = order % capacity
    onehot = (target_dev[:, :, None] == jnp.arange(peers, dtype=jnp.int32)).astype(BF16)
    earlier = (jnp.arange(capacity)[:, None] > jnp.arange(capacity)[None, :]).astype(BF16)
    before = jnp.stack([dot(earlier, onehot[m]) for m in range(batches)])
    rank_in = jnp.sum(before * onehot.astype(F32), axis=2).astype(jnp.int32)
    send_slot = target_dev * group_rows + rank_in
    my_slot = lax.dynamic_index_in_dim(send_slot, mine, 0, keepdims=False)
    my_row = lax.dynamic_index_in_dim(local_row, mine, 0, keepdims=False)
    my_tokens = lax.dynamic_index_in_dim(tokens, mine, 0, keepdims=False)
    my_cot = lax.dynamic_index_in_dim(cotangent, mine, 0, keepdims=False)
    my_counts = lax.dynamic_index_in_dim(lengths, mine, 0, keepdims=False)[0]
    shape_three = (peers, group_rows, model_width)
    pick = (jnp.arange(capacity, dtype=jnp.int32)[:, None] == my_slot[None, :])
    send_rows = dot(pick.astype(BF16), my_tokens).astype(BF16).reshape(shape_three)
    send_cot = dot(pick.astype(BF16), my_cot).astype(BF16).reshape(shape_three)
    send_index = jnp.sum(jnp.where(pick, my_row[None, :], 0), axis=1).reshape(peers, 1, group_rows)
    send_index = jnp.pad(send_index, ((0, 0), (0, 7), (0, LANES - group_rows)))
    recv_rows, recv_cot, recv_index, full_a, full_b, full_bias = head(
        send_rows, send_cot, send_index, shard_a, shard_b, bias, peers
    )
    recv_rows = recv_rows.reshape(capacity, model_width)
    recv_cot = recv_cot.reshape(capacity, model_width)
    recv_index = recv_index[:, 0, :group_rows].reshape(capacity)
    full_a = full_a.reshape(partners, model_width, -1)
    full_b = full_b.reshape(partners, model_width, -1)
    full_bias = full_bias.reshape(partners, -1)
    q_bias = full_bias[:, :local_width]
    v_bias = full_bias[:, local_width : 2 * local_width]
    up_full_bias = full_bias[:, 2 * local_width : 2 * local_width + hidden_width]
    block_rows = select(recv_index, recv_rows)
    block_cot = select(recv_index, recv_cot)

    places = jnp.arange(capacity, dtype=jnp.int32)
    seg_ends = jnp.cumsum(my_counts)
    segment = jnp.sum((places[:, None] >= seg_ends[None, :]).astype(jnp.int32), axis=1)
    valid_rows = (places < seg_ends[-1]).astype(F32)
    tag = jnp.arange(LANES, dtype=jnp.int32) % (LANES // 2)
    same = segment[:, None] == tag[None, :]
    tags_q = same.astype(BF16)
    tags_k = jnp.where(
        tag[None, :] < slots, jnp.where(same, 0.0, NEGATIVE), (tag[None, :] < slots + 3).astype(F32)
    ).astype(BF16)

    mixed_bias = jnp.concatenate([q_bias, jnp.zeros_like(q_bias), v_bias], axis=1)
    qkv = jnp.stack(
        [
            (dot(block_rows, full_a[t, :, :attn_cols]) + mixed_bias[t]).astype(BF16)
            for t in range(partners)
        ]
    )
    context, keep = attend(qkv, tags_q, tags_k, slots)
    attended = sum(dot(context[t], full_a[t, :, attn_cols:], NT) for t in range(partners))
    first, normed_one, inverse_one = normalize(
        block_rows.astype(F32) + attended + out_bias, gain_one, shift_one
    )
    hidden = first.astype(BF16)
    up_value = [dot(hidden, full_b[t, :, :hidden_width]) + up_full_bias[t] for t in range(partners)]
    active = [jax.nn.gelu(u, approximate=False).astype(BF16) for u in up_value]
    branch = sum(dot(active[t], full_b[t, :, hidden_width:], NT) for t in range(partners))
    second, normed_two, inverse_two = normalize(
        hidden.astype(F32) + branch + down_bias, gain_two, shift_two
    )
    layout_out = (second * valid_rows[:, None]).astype(BF16)

    grad_y = block_cot.astype(F32) * valid_rows[:, None]
    grad_second, gain_two_part, shift_two_part = normalize_back(
        grad_y, normed_two, inverse_two, gain_two
    )
    grad_branch = grad_second.astype(BF16)
    hidden_terms = 0.0
    up_bias_part = []
    grad_ups = []
    for t in range(partners):
        grad_active = dot(grad_branch, full_b[t, :, hidden_width:])
        u = up_value[t]
        slope = 0.5 * (1.0 + lax.erf(u * SQRT_HALF)) + u * jnp.exp(-0.5 * u * u) * INV_ROOT_TAU
        grad_up = (grad_active * slope).astype(BF16)
        grad_ups.append(grad_up)
        up_bias_part.append(jnp.sum(grad_up.astype(F32), axis=0))
        hidden_terms = hidden_terms + dot(grad_up, full_b[t, :, :hidden_width], NT)

    def weight_grad(left, right):
        grad = jnp.einsum("rd,trf->tdf", left, jnp.stack(right), preferred_element_type=BF16)
        return grad.reshape(partners, peers, shard_rows, -1)

    up_grad = weight_grad(hidden, grad_ups)
    down_grad = weight_grad(grad_branch, active)
    grad_hidden = grad_second + hidden_terms
    grad_first, gain_one_part, shift_one_part = normalize_back(
        grad_hidden, normed_one, inverse_one, gain_one
    )
    grad_attended = grad_first.astype(BF16)
    grad_context = jnp.stack(
        [dot(grad_attended, full_a[t, :, attn_cols:], out=F32).astype(BF16) for t in range(partners)]
    )
    grad_q, grad_k, grad_v = attend_back(qkv, keep, context, grad_context, tags_k)
    input_terms = grad_first
    mixed_grads = []
    for t in range(partners):
        grad_mixed = jnp.concatenate([grad_q[t], grad_k[t], grad_v[t]], axis=1)
        mixed_grads.append(grad_mixed)
        input_terms = input_terms + dot(grad_mixed, full_a[t, :, :attn_cols], NT)
    attn_grad = weight_grad(block_rows, mixed_grads)
    out_grad = weight_grad(grad_attended, [context[t] for t in range(partners)])
    layout_grad = input_terms.astype(BF16)
    small = jnp.concatenate(
        [
            jnp.sum(grad_q.astype(F32), axis=1).reshape(-1),
            jnp.sum(grad_v.astype(F32), axis=1).reshape(-1),
            jnp.concatenate(up_bias_part),
            jnp.sum(grad_first, axis=0),
            gain_one_part,
            shift_one_part,
            jnp.sum(grad_second, axis=0),
            gain_two_part,
            shift_two_part,
        ]
    )
    exchange = functools.partial(
        lax.all_to_all, axis_name="dp", split_axis=0, concat_axis=0, tiled=True
    )
    back_out = exchange(select_back(recv_index, layout_out).reshape(shape_three))
    back_grad = select_back(recv_index, layout_grad).reshape(shape_three)
    home_grad, small, attn_share, out_share, up_share, down_share = tail(
        back_grad, small.reshape(-1, LANES), [attn_grad, out_grad, up_grad, down_grad], peers
    )
    small = small.reshape(-1)
    width = model_width
    ends = [0, width, 2 * width]
    q_sum = small[:width].reshape(partners, -1)
    v_sum = small[width : 2 * width].reshape(partners, -1)
    base = 2 * width + partners * hidden_width
    u_sum = small[2 * width : base].reshape(partners, -1)
    rest = small[base:].reshape(6, width)
    own = functools.partial(lax.dynamic_index_in_dim, index=mine, axis=0, keepdims=False)

    swap = [(i, (i + 1) % partners) for i in range(partners)]

    def home(back):
        here = back.reshape(capacity, model_width)
        there = lax.ppermute(here, "tensor", swap)
        rows = []
        for m in range(batches):
            rows.append(select_back(send_slot[m], jnp.where(mine == m, here, there)))
        return jnp.stack(rows)

    output = home(back_out)
    input_grad = jnp.stack(
        [select_back(send_slot[m], home_grad[m].reshape(capacity, model_width)) for m in range(batches)]
    )
    return (
        output,
        input_grad,
        attn_share.reshape(shard_rows, 3, local_width),
        jnp.stack([own(q_sum), own(v_sum)]),
        out_share.T,
        rest[0],
        rest[1],
        rest[2],
        up_share,
        own(u_sum),
        down_share.T,
        rest[3],
        rest[4],
        rest[5],
    )


def solution(mesh):
    in_specs = (
        P(None, "dp", None),
        P(None, "dp"),
        P(None, "dp", None),
        P("dp", None, "tensor"),
        P(None, "tensor"),
        P("tensor", "dp"),
        P(),
        P(),
        P(),
        P("dp", "tensor"),
        P("tensor"),
        P("tensor", "dp"),
        P(),
        P(),
        P(),
        P(None, "dp", None),
    )
    out_specs = (
        P(None, "dp", None),
        P(None, "dp", None),
        P("dp", None, "tensor"),
        P(None, "tensor"),
        P("tensor", "dp"),
        P(),
        P(),
        P(),
        P("dp", "tensor"),
        P("tensor"),
        P("tensor", "dp"),
        P(),
        P(),
        P(),
    )
    return jax.shard_map(
        per_device, mesh=mesh, in_specs=in_specs, out_specs=out_specs, check_vma=False
    )
```
